32 devices in a mesh: groups: 2 (over y), rep: 4 (over x, core), tp: 4 (over z).
Axes of the slice: x: 2, y: 2, z: 4, core: 2. Of those that a mesh axis runs over, the one named last changes fastest.
Arguments:
- tokens: bfloat16 [3072, 8192], P(('groups', 'rep', 'tp')), parts along dimension 0, may hold values from -6 to 6
- base_weight: bfloat16 [8192, 2048], P(None, 'tp'), may hold values from -0.0625 to 0.0625
- delta_codes: bfloat16 [32768, 2048], P(('groups', 'rep'), 'tp'), parts along dimension 0, may hold values from -4 to 4
- delta_scales: bfloat16 [256, 16], P(('groups', 'rep'), 'tp'), parts along dimension 0, may hold values from 0.0019989014 to 0.011962891
- replica_variant: int32 [8], P('groups'), parts along dimension 0, may hold values from 0 to 1
- block_home: int32 [4, 64], P('groups'), parts along dimension 0, may hold values from 0 to 127, as said below
Outputs:
- key_value: bfloat16 [3072, 2048], P(('groups', 'rep'), 'tp'), parts along dimension 0
The draws below stay inside these ranges and needn't reach their ends.
There are 2 independent parts, one for each index of `groups`. The reference program is written for one: setup_inputs(seed, part) draws one part's arguments, and reference() takes and returns one part's arrays. A program takes and returns all parts, laid end to end along the dimension named above; an argument that names none is the same for every part. Nothing has to cross between parts.
Inputs may be any that keep to these rules, and one draw needn't show every extreme that they name: `block_home`: the entries are a permutation of 0 to 127; entry e stands for slot e % 32 of holder e // 32, that is rows e * 128 to (e + 1) * 128 - 1 of delta_codes. At most 24 blocks of one variant lie with one holder, and in every draw some holders hold exactly 24 blocks of a variant.
All inputs are finite; a program needn't handle non-finite values.
Results may differ from the reference program's by a relative error of at most 0.0049.
Values may be sent and summed in bfloat16 or wider, within the bound.
A program may use at most 128 MiB of HBM per device.

```python
import math
import jax
import jax.numpy as jnp
from jax import lax

D = 8192
BLOCK = 128
HOLDERS = 4
VARIANTS = 2
NB = 64
SLOTS = 32
COLS = 2048
TOK = 384


def draw_block_home(key, part):
    first, second, third = jax.random.split(jax.random.fold_in(key, 7), 3)
    sigma = jax.random.permutation(first, HOLDERS)
    share = NB // HOLDERS
    swing = share // 2
    rows_index = jnp.arange(VARIANTS)
    holder_index = jnp.arange(HOLDERS)
    plus_hot = (holder_index[None, :] == sigma[2 * rows_index][:, None]).astype(jnp.int32)
    minus_hot = (holder_index[None, :] == sigma[2 * rows_index + 1][:, None]).astype(jnp.int32)
    change = plus_hot - minus_hot
    change = change - jnp.roll(change, 1, axis=0)
    counts = share + swing * change

    def spread(count_row):
        return jnp.repeat(holder_index, count_row, total_repeat_length=NB)
    holder_lists = jax.vmap(spread)(counts)
    variant_keys = jax.random.split(second, VARIANTS)
    holder_lists = jax.vmap(jax.random.permutation)(variant_keys, holder_lists)
    flat_holders = holder_lists.reshape(-1).astype(jnp.int32)
    shuffle = jax.random.permutation(third, VARIANTS * NB).astype(jnp.int32)
    score = flat_holders * (VARIANTS * NB) + shuffle
    sorted_index = jnp.argsort(score)
    ranks = jnp.zeros((VARIANTS * NB,), jnp.int32).at[sorted_index].set(jnp.arange(VARIANTS * NB, dtype=jnp.int32))
    return ranks.reshape(VARIANTS, NB)


def plant(array, rng, least, high):
    shape = array.shape
    place = [jax.random.randint(jax.random.fold_in(rng, axis), (), 0, shape[axis]) for axis in range(len(shape))]
    array = array.at[tuple(place)].set(least)
    longest = shape.index(max(shape))
    place[longest] = (place[longest] + 1) % shape[longest]
    return array.at[tuple(place)].set(high)


def block_scale(rng, dims, shards, least, top_value):
    def one(dim, blocks):
        steps = jax.random.uniform(jax.random.fold_in(jax.random.fold_in(rng, 6), dim), (blocks,), jnp.float32, least / len(shards), top_value / len(shards))
        return jnp.repeat(jnp.exp(steps), dims[dim] // blocks).reshape((-1,) + (1,) * (len(dims) - dim - 1))

    gain = one(*shards[0])
    for cut in shards[1:]:
        gain = gain * one(*cut)
    return gain


def scatter_about(own_key, dims, scale, reach, cuts=(), kind=jnp.bfloat16):
    loudness = block_scale(own_key, dims, cuts, -0.22, 0.18) if cuts else 1.0
    array = jax.random.normal(own_key, dims, jnp.float32) * scale * loudness
    return jnp.minimum(jnp.maximum(array, -reach), reach).astype(kind)


def setup_inputs(seed: int = 0, part: int = 0) -> dict:
    splits = jax.random.split(jax.random.key(seed), 7)
    part_splits = jax.random.split(jax.random.fold_in(splits[6], part), 7)
    tokens = scatter_about(part_splits[0], (HOLDERS * TOK, D), 1.0, 6.0, ((0, 16),))
    base_weight = scatter_about(splits[1], (D, COLS), D ** -0.5, 0.0625, ((1, 4),))
    delta_codes = scatter_about(part_splits[2], (HOLDERS * SLOTS * BLOCK, COLS), 1.0, 4.0, ((0, 4), (1, 4)))
    delta_scales = jnp.clip(jnp.exp(math.log(0.011962891) - 1.7892117 * jax.random.uniform(part_splits[3], (HOLDERS * SLOTS, COLS // BLOCK), jnp.float32) ** block_scale(part_splits[3], (HOLDERS * SLOTS, COLS // BLOCK), ((0, 4), (1, 4)), -0.2, 0.2)), 0.0019989014, 0.011962891).astype(jnp.bfloat16)
    replica_variant = plant(jax.random.randint(part_splits[4], (HOLDERS,), 0, VARIANTS), jax.random.fold_in(part_splits[4], 1), 0, VARIANTS - 1).astype(jnp.int32)
    block_home = draw_block_home(jax.random.fold_in(jax.random.fold_in(splits[6], part), 71), part)
    return dict(tokens=tokens, base_weight=base_weight, delta_codes=delta_codes, delta_scales=delta_scales, replica_variant=replica_variant, block_home=block_home)


def reference(tokens, base_weight, delta_codes, delta_scales, replica_variant, block_home):
    code_blocks = delta_codes.reshape(HOLDERS * SLOTS, BLOCK, COLS)
    col_blocks = COLS // BLOCK
    base_float = base_weight.astype(jnp.float32)
    prompts = tokens.reshape(HOLDERS, TOK, D)

    def project_one(inputs_pair):
        prompt, variant = inputs_pair
        homes = block_home[variant]
        code_vals = code_blocks[homes].astype(jnp.float32)
        scales = delta_scales[homes].astype(jnp.float32)
        scale_full = jnp.broadcast_to(scales[:, None, :, None], (NB, BLOCK, col_blocks, BLOCK)).reshape(NB, BLOCK, COLS)
        weight = (base_float + (code_vals * scale_full).reshape(D, COLS)).astype(jnp.bfloat16)
        return jnp.dot(prompt, weight, preferred_element_type=jnp.float32).astype(jnp.bfloat16)

    outputs = lax.map(project_one, (prompts, replica_variant))
    return outputs.reshape(HOLDERS * TOK, COLS)
```

```python
import functools

import jax
import jax.numpy as jnp
from jax import lax
from jax.experimental import pallas as pl
from jax.experimental.pallas import tpu as pltpu
from jax.sharding import PartitionSpec as P

MESH = pl.DeviceIdType.MESH


def kernel(
    geo, variant_ref, home_ref, scale_ref, tok_ref, base_ref, code_ref, out_ref,
    tok_buf, code_buf, base_buf, scale_buf, scale_full, total,
    tok_send, tok_recv, code_send, code_recv, scale_send, scale_recv, local_sem,
):
    tps, reps, tok_parts, code_parts, slots, block, width = geo
    chips = reps // 2
    rep = lax.axis_index("rep")
    tp = lax.axis_index("tp")
    core = lax.rem(rep, 2)
    chip = rep // 2
    partner = {"rep": rep + 1 - 2 * core}
    depth = tok_ref.shape[1]
    tok_step = depth // tok_parts
    code_step = slots // code_parts

    own = [
        pltpu.make_async_copy(code_ref, code_buf.at[pl.ds(rep * slots, slots)], local_sem.at[0]),
        pltpu.make_async_copy(tok_ref, tok_buf.at[tp], local_sem.at[1]),
        pltpu.make_async_copy(base_ref, base_buf, local_sem.at[2]),
        pltpu.make_async_copy(scale_ref, scale_buf.at[rep], local_sem.at[3]),
    ]

    barrier = pltpu.get_barrier_semaphore()

    def greet(device):
        pl.semaphore_signal(barrier, inc=1, device_id=device, device_id_type=MESH)

    greet(partner)
    sides = []
    for axis, me, place, stride, count in (("tp", tp, tp, 1, tps), ("rep", rep, chip, 2, chips)):
        up = (place < count - 1, {axis: me + stride})
        down = (place > 0, {axis: me - stride})
        for there, device in (up, down):
            pl.when(there)(functools.partial(greet, device))
        sides.append((up, down))
    (tok_up, tok_down), (code_up, code_down) = sides
    met = 1 + sum(there.astype(jnp.int32) for there, _ in (tok_up, tok_down, code_up, code_down))
    pl.semaphore_wait(barrier, met)

    def tok_copy(src, owner, part, way, hop, device):
        cols = pl.ds(part * tok_step, tok_step)
        return pltpu.make_async_remote_copy(
            src_ref=tok_ref.at[:, cols] if src is None else tok_buf.at[owner, :, cols],
            dst_ref=tok_buf.at[owner, :, cols],
            send_sem=tok_send.at[way, hop, part],
            recv_sem=tok_recv.at[owner, part],
            device_id=device,
            device_id_type=MESH,
        )

    def code_copy(src, owner, part, way, hop, device):
        rows = pl.ds(owner * slots + part * code_step, code_step)
        return pltpu.make_async_remote_copy(
            src_ref=code_ref.at[pl.ds(part * code_step, code_step)] if src is None else code_buf.at[rows],
            dst_ref=code_buf.at[rows],
            send_sem=code_send.at[way, hop, part],
            recv_sem=code_recv.at[owner, part],
            device_id=device,
            device_id_type=MESH,
        )

    def scale_copy(src, owner, way, hop, device):
        return pltpu.make_async_remote_copy(
            src_ref=scale_ref if src is None else scale_buf.at[owner],
            dst_ref=scale_buf.at[owner],
            send_sem=scale_send.at[way, hop],
            recv_sem=scale_recv.at[owner],
            device_id=device,
            device_id_type=MESH,
        )

    for way, (there, device) in enumerate((code_up, code_down)):
        @pl.when(there)
        def _():
            scale_copy(None, rep, way, 0, device).start()
            for part in range(code_parts):
                code_copy(None, rep, part, way, 0, device).start()

    for way, (there, device) in enumerate((tok_up, tok_down)):
        @pl.when(there)
        def _():
            for part in range(tok_parts):
                tok_copy(None, tp, part, way, 0, device).start()

    scale_copy(None, rep, 2, 0, partner).start()
    for part in range(code_parts):
        code_copy(None, rep, part, 2, 0, partner).start()
    for copy in own:
        copy.start()

    events = [
        ((hop * tok_parts + part + 1) * tok_ref.shape[0] * tok_step, 0, hop, part)
        for hop in range(tps - 1) for part in range(tok_parts)
    ] + [
        ((hop * code_parts + part + 1) * code_step * block * width, 1, hop, part)
        for hop in range(chips - 1) for part in range(code_parts)
    ]
    for _, kind, hop, part in sorted(events):
        for way in range(2):
            sign = 1 - 2 * way
            if kind == 0:
                place, count = tp, tps
                origin = tp - sign * (hop + 1)
                owner = origin
                onward = (tok_up, tok_down)[way]
            else:
                place, count = chip, chips
                origin = chip - sign * (hop + 1)
                owner = rep - 2 * sign * (hop + 1)
                onward = (code_up, code_down)[way]

            @pl.when((origin >= 0) & (origin < count))
            def _():
                if kind == 0:
                    tok_copy(1, owner, part, way, 0, partner).wait_recv()
                    if hop < tps - 2:
                        @pl.when(onward[0])
                        def _():
                            tok_copy(1, owner, part, way, hop + 1, onward[1]).start()
                else:
                    if part == 0:
                        scale_copy(1, owner, way, 0, partner).wait_recv()
                    code_copy(1, owner, part, way, 0, partner).wait_recv()
                    if part == 0:
                        scale_copy(1, owner, 2 + way, hop + 1, partner).start()
                    code_copy(1, owner, part, 2 + way, hop + 1, partner).start()
                    if hop < chips - 2:
                        @pl.when(onward[0])
                        def _():
                            if part == 0:
                                scale_copy(1, owner, way, hop + 1, onward[1]).start()
                            code_copy(1, owner, part, way, hop + 1, onward[1]).start()

    for other in range(chips):
        owner = 2 * other + 1 - core
        scale_copy(1, owner, 0, 0, partner).wait_recv()
        for part in range(code_parts):
            code_copy(1, owner, part, 0, 0, partner).wait_recv()
    for copy in own:
        copy.wait()

    for owner in range(reps):
        scales = scale_buf[owner].astype(jnp.float32)
        for col in range(scales.shape[1]):
            scale_full[owner * slots:(owner + 1) * slots, col * block:(col + 1) * block] = (
                jnp.broadcast_to(scales[:, col:col + 1], (slots, block))
            )

    variant = variant_ref[rep]
    group = 4
    total[...] = jnp.zeros_like(total)

    def multiply(step, carry):
        merged = []
        for i in range(group):
            b = step * group + i
            e = home_ref[variant, b]
            delta = code_buf[e].astype(jnp.float32) * scale_full[pl.ds(e, 1), :]
            rows = pl.ds(pl.multiple_of(b * block, block), block)
            merged.append((base_buf[rows, :].astype(jnp.float32) + delta).astype(jnp.bfloat16))
        span = group * block
        cols = pl.ds(pl.multiple_of(step * span, span), span)
        prompt = tok_buf[:, :, cols].reshape(total.shape[0], span)
        total[...] += jnp.dot(prompt, jnp.concatenate(merged, axis=0), preferred_element_type=jnp.float32)
        return carry

    lax.fori_loop(0, depth // (group * block), multiply, 0)
    out_ref[...] = total[...].astype(out_ref.dtype)

    for way, (there, device) in enumerate((tok_up, tok_down)):
        for hop in range(tps - 1):
            origin = tp - (1 - 2 * way) * hop

            @pl.when(there & (origin >= 0) & (origin < tps))
            def _():
                for part in range(tok_parts):
                    tok_copy(1, origin, part, way, hop, device).wait_send()
    for way, (there, device) in enumerate((code_up, code_down)):
        sign = 1 - 2 * way
        for hop in range(chips):
            origin = chip - sign * hop
            owner = rep - 2 * sign * hop
            here = (origin >= 0) & (origin < chips)
            if hop < chips - 1:
                @pl.when(there & here)
                def _():
                    scale_copy(1, owner, way, hop, device).wait_send()
                    for part in range(code_parts):
                        code_copy(1, owner, part, way, hop, device).wait_send()
            if hop or not way:
                @pl.when(here)
                def _():
                    scale_copy(1, owner, 2 + way, hop, partner).wait_send()
                    for part in range(code_parts):
                        code_copy(1, owner, part, 2 + way, hop, partner).wait_send()


def local(tps, reps, tokens, base_weight, delta_codes, delta_scales, replica_variant, block_home):
    slots, col_blocks = delta_scales.shape
    rows, depth = tokens.shape
    width = base_weight.shape[1]
    block = delta_codes.shape[0] // slots
    tok_parts = max(1, 16 // tps)
    code_parts = max(1, 32 // reps)
    codes = delta_codes.reshape(slots, block, width)
    dma = pltpu.SemaphoreType.DMA
    chips = reps // 2
    return pl.pallas_call(
        functools.partial(kernel, (tps, reps, tok_parts, code_parts, slots, block, width)),
        out_shape=jax.ShapeDtypeStruct((tps * rows, width), jnp.bfloat16),
        in_specs=[pl.BlockSpec(memory_space=pltpu.SMEM)] * 2
        + [pl.BlockSpec(memory_space=pltpu.VMEM)]
        + [pl.BlockSpec(memory_space=pl.ANY)] * 3,
        out_specs=pl.BlockSpec(memory_space=pltpu.VMEM),
        scratch_shapes=[
            pltpu.VMEM((tps, rows, depth), jnp.bfloat16),
            pltpu.VMEM((reps * slots, block, width), jnp.bfloat16),
            pltpu.VMEM((depth, width), jnp.bfloat16),
            pltpu.VMEM((reps, slots, col_blocks), jnp.bfloat16),
            pltpu.VMEM((reps * slots, width), jnp.float32),
            pltpu.VMEM((tps * rows, width), jnp.float32),
            dma((2, tps, tok_parts)),
            dma((tps, tok_parts)),
            dma((4, chips, code_parts)),
            dma((reps, code_parts)),
            dma((4, chips)),
            dma((reps,)),
            dma((4,)),
        ],
        compiler_params=pltpu.CompilerParams(
            collective_id=0, has_side_effects=True, vmem_limit_bytes=60 * 1024 * 1024
        ),
    )(replica_variant, block_home, delta_scales, tokens, base_weight, codes)


def solution(mesh):
    in_specs = (
        P(("groups", "rep", "tp"), None),
        P(None, "tp"),
        P(("groups", "rep"), "tp"),
        P(("groups", "rep"), "tp"),
        P("groups"),
        P("groups", None),
    )
    out_specs = P(("groups", "rep"), "tp")
    body = functools.partial(local, mesh.shape["tp"], mesh.shape["rep"])
    return jax.shard_map(body, mesh=mesh, in_specs=in_specs, out_specs=out_specs, check_vma=False)
```

```python
import functools

import jax
import jax.numpy as jnp
from jax import lax
from jax.experimental import pallas as pl
from jax.experimental.pallas import tpu as pltpu
from jax.sharding import PartitionSpec as P

MESH = pl.DeviceIdType.MESH


def kernel(
    geo, variant_ref, home_ref, scale_ref, tok_ref, base_ref, code_ref, out_ref,
    tok_buf, code_buf, base_buf, scale_buf, scale_full, total,
    tok_send, tok_recv, code_send, code_recv, scale_send, scale_recv, local_sem,
):
    tps, reps, tok_parts, code_parts, slots, block, width = geo
    chips = reps // 2
    rep = lax.axis_index("rep")
    tp = lax.axis_index("tp")
    core = lax.rem(rep, 2)
    chip = rep // 2
    partner = {"rep": rep + 1 - 2 * core}
    depth = tok_ref.shape[1]
    tok_step = depth // tok_parts
    code_step = slots // code_parts

    own = [
        pltpu.make_async_copy(code_ref, code_buf.at[pl.ds(rep * slots, slots)], local_sem.at[0]),
        pltpu.make_async_copy(tok_ref, tok_buf.at[tp], local_sem.at[1]),
        pltpu.make_async_copy(base_ref, base_buf, local_sem.at[2]),
        pltpu.make_async_copy(scale_ref, scale_buf.at[rep], local_sem.at[3]),
    ]

    barrier = pltpu.get_barrier_semaphore()

    def greet(device):
        pl.semaphore_signal(barrier, inc=1, device_id=device, device_id_type=MESH)

    greet(partner)
    sides = []
    for axis, me, place, stride, count in (("tp", tp, tp, 1, tps), ("rep", rep, chip, 2, chips)):
        up = (place < count - 1, {axis: me + stride})
        down = (place > 0, {axis: me - stride})
        for there, device in (up, down):
            pl.when(there)(functools.partial(greet, device))
        sides.append((up, down))
    (tok_up, tok_down), (code_up, code_down) = sides
    met = 1 + sum(there.astype(jnp.int32) for there, _ in (tok_up, tok_down, code_up, code_down))
    pl.semaphore_wait(barrier, met)

    def tok_copy(src, owner, part, way, hop, device):
        cols = pl.ds(part * tok_step, tok_step)
        return pltpu.make_async_remote_copy(
            src_ref=tok_ref.at[:, cols] if src is None else tok_buf.at[owner, :, cols],
            dst_ref=tok_buf.at[owner, :, cols],
            send_sem=tok_send.at[way, hop, part],
            recv_sem=tok_recv.at[owner, part],
            device_id=device,
            device_id_type=MESH,
        )

    def code_copy(src, owner, part, way, hop, device):
        rows = pl.ds(owner * slots + part * code_step, code_step)
        return pltpu.make_async_remote_copy(
            src_ref=code_ref.at[pl.ds(part * code_step, code_step)] if src is None else code_buf.at[rows],
            dst_ref=code_buf.at[rows],
            send_sem=code_send.at[way, hop, part],
            recv_sem=code_recv.at[owner, part],
            device_id=device,
            device_id_type=MESH,
        )

    def scale_copy(src, owner, way, hop, device):
        return pltpu.make_async_remote_copy(
            src_ref=scale_ref if src is None else scale_buf.at[owner],
            dst_ref=scale_buf.at[owner],
            send_sem=scale_send.at[way, hop],
            recv_sem=scale_recv.at[owner],
            device_id=device,
            device_id_type=MESH,
        )

    for way, (there, device) in enumerate((tok_up, tok_down)):
        @pl.when(there)
        def _():
            for part in range(tok_parts):
                tok_copy(None, tp, part, way, 0, device).start()

    for way, (there, device) in enumerate((code_up, code_down)):
        @pl.when(there)
        def _():
            scale_copy(None, rep, way, 0, device).start()
            for part in range(code_parts):
                code_copy(None, rep, part, way, 0, device).start()

    scale_copy(None, rep, 2, 0, partner).start()
    for part in range(code_parts):
        code_copy(None, rep, part, 2, 0, partner).start()
    for copy in own:
        copy.start()

    events = [
        ((hop * tok_parts + part + 1) * tok_ref.shape[0] * tok_step, 0, hop, part)
        for hop in range(tps - 2) for part in range(tok_parts)
    ] + [
        ((hop * code_parts + part + 1) * code_step * block * width, 1, hop, part)
        for hop in range(chips - 1) for part in range(code_parts)
    ]
    for _, kind, hop, part in sorted(events):
        for way in range(2):
            sign = 1 - 2 * way
            if kind == 0:
                place, count = tp, tps
                origin = tp - sign * (hop + 1)
                owner = origin
                onward = (tok_up, tok_down)[way]
            else:
                place, count = chip, chips
                origin = chip - sign * (hop + 1)
                owner = rep - 2 * sign * (hop + 1)
                onward = (code_up, code_down)[way]

            @pl.when((origin >= 0) & (origin < count))
            def _():
                if kind == 0:
                    tok_copy(1, owner, part, way, 0, partner).wait_recv()
                    @pl.when(onward[0])
                    def _():
                        tok_copy(1, owner, part, way, hop + 1, onward[1]).start()
                else:
                    if part == 0:
                        scale_copy(1, owner, way, 0, partner).wait_recv()
                    code_copy(1, owner, part, way, 0, partner).wait_recv()
                    if part == 0:
                        scale_copy(1, owner, 2 + way, hop + 1, partner).start()
                    code_copy(1, owner, part, 2 + way, hop + 1, partner).start()
                    if hop < chips - 2:
                        @pl.when(onward[0])
                        def _():
                            if part == 0:
                                scale_copy(1, owner, way, hop + 1, onward[1]).start()
                            code_copy(1, owner, part, way, hop + 1, onward[1]).start()

    for other in range(chips):
        owner = 2 * other + 1 - core
        scale_copy(1, owner, 0, 0, partner).wait_recv()
        for part in range(code_parts):
            code_copy(1, owner, part, 0, 0, partner).wait_recv()
    for copy in own:
        copy.wait()

    slot_row = lax.broadcasted_iota(jnp.int32, (slots, slots), 0)
    diagonal = slot_row == lax.broadcasted_iota(jnp.int32, (slots, slots), 1)
    for owner in range(reps):
        scales = scale_buf[owner].astype(jnp.float32)
        for col in range(scales.shape[0]):
            across = jnp.broadcast_to(scales[col:col + 1, :], (slots, slots))
            down = jnp.sum(jnp.where(diagonal, across, 0.0), axis=1, keepdims=True)
            scale_full[owner * slots:(owner + 1) * slots, col * block:(col + 1) * block] = (
                jnp.broadcast_to(down, (slots, block))
            )

    variant = variant_ref[rep]
    rows = tok_ref.shape[0]
    group = 4
    span = group * block

    def merge_and_multiply(first, shards):
        here = pl.ds(0, shards * rows)
        total[here, :] = jnp.zeros((shards * rows, width), jnp.float32)

        def step(at, carry):
            merged = []
            for i in range(group):
                b = at * group + i
                e = home_ref[variant, b]
                delta = code_buf[e].astype(jnp.float32) * scale_full[pl.ds(e, 1), :]
                lines = pl.ds(pl.multiple_of(b * block, block), block)
                merged.append((base_buf[lines, :].astype(jnp.float32) + delta).astype(jnp.bfloat16))
            merged = jnp.concatenate(merged, axis=0)
            cols = pl.ds(pl.multiple_of(at * span, span), span)
            if shards < tps:
                base_buf[cols, :] = merged
            prompt = tok_buf[pl.ds(first, shards), :, cols].reshape(shards * rows, span)
            total[here, :] += jnp.dot(prompt, merged, preferred_element_type=jnp.float32)
            return carry

        lax.fori_loop(0, depth // span, step, 0)
        out_ref[pl.ds(pl.multiple_of(first * rows, rows), shards * rows), :] = total[here, :].astype(out_ref.dtype)

    at_end = (tp == 0) | (tp == tps - 1)

    @pl.when(at_end)
    def _():
        merge_and_multiply((tp > 0).astype(jnp.int32), tps - 1)
        far = tps - 1 - tp
        last = pl.ds(0, rows)
        total[last, :] = jnp.zeros((rows, width), jnp.float32)
        for part in range(tok_parts):
            tok_copy(1, far, part, 0, 0, partner).wait_recv()

            def step(at, carry):
                cols = pl.ds(pl.multiple_of(part * tok_step + at * span, span), span)
                total[last, :] += jnp.dot(tok_buf[far, :, cols], base_buf[cols, :], preferred_element_type=jnp.float32)
                return carry

            lax.fori_loop(0, tok_step // span, step, 0)
        out_ref[pl.ds(pl.multiple_of(far * rows, rows), rows), :] = total[last, :].astype(out_ref.dtype)

    @pl.when(jnp.logical_not(at_end))
    def _():
        merge_and_multiply(0, tps)

    for way, (there, device) in enumerate((tok_up, tok_down)):
        for hop in range(tps - 1):
            origin = tp - (1 - 2 * way) * hop

            @pl.when(there & (origin >= 0) & (origin < tps))
            def _():
                for part in range(tok_parts):
                    tok_copy(1, origin, part, way, hop, device).wait_send()
    for way, (there, device) in enumerate((code_up, code_down)):
        sign = 1 - 2 * way
        for hop in range(chips):
            origin = chip - sign * hop
            owner = rep - 2 * sign * hop
            here = (origin >= 0) & (origin < chips)
            if hop < chips - 1:
                @pl.when(there & here)
                def _():
                    scale_copy(1, owner, way, hop, device).wait_send()
                    for part in range(code_parts):
                        code_copy(1, owner, part, way, hop, device).wait_send()
            if hop or not way:
                @pl.when(here)
                def _():
                    scale_copy(1, owner, 2 + way, hop, partner).wait_send()
                    for part in range(code_parts):
                        code_copy(1, owner, part, 2 + way, hop, partner).wait_send()


def local(tps, reps, tokens, base_weight, delta_codes, delta_scales, replica_variant, block_home):
    slots, col_blocks = delta_scales.shape
    rows, depth = tokens.shape
    width = base_weight.shape[1]
    block = delta_codes.shape[0] // slots
    tok_parts = max(1, 32 // tps)
    code_parts = max(1, 32 // reps)
    codes = delta_codes.reshape(slots, block, width)
    dma = pltpu.SemaphoreType.DMA
    chips = reps // 2
    return pl.pallas_call(
        functools.partial(kernel, (tps, reps, tok_parts, code_parts, slots, block, width)),
        out_shape=jax.ShapeDtypeStruct((tps * rows, width), jnp.bfloat16),
        in_specs=[pl.BlockSpec(memory_space=pltpu.SMEM)] * 2
        + [pl.BlockSpec(memory_space=pl.ANY)] * 4,
        out_specs=pl.BlockSpec(memory_space=pltpu.VMEM),
        scratch_shapes=[
            pltpu.VMEM((tps, rows, depth), jnp.bfloat16),
            pltpu.VMEM((reps * slots, block, width), jnp.bfloat16),
            pltpu.VMEM((depth, width), jnp.bfloat16),
            pltpu.VMEM((reps, col_blocks, slots), jnp.bfloat16),
            pltpu.VMEM((reps * slots, width), jnp.float32),
            pltpu.VMEM((tps * rows, width), jnp.float32),
            dma((2, tps, tok_parts)),
            dma((tps, tok_parts)),
            dma((4, chips, code_parts)),
            dma((reps, code_parts)),
            dma((4, chips)),
            dma((reps,)),
            dma((4,)),
        ],
        compiler_params=pltpu.CompilerParams(
            collective_id=0, has_side_effects=True, vmem_limit_bytes=60 * 1024 * 1024
        ),
    )(replica_variant, block_home, delta_scales.T, tokens, base_weight, codes)


def solution(mesh):
    in_specs = (
        P(("groups", "rep", "tp"), None),
        P(None, "tp"),
        P(("groups", "rep"), "tp"),
        P(("groups", "rep"), "tp"),
        P("groups"),
        P("groups", None),
    )
    out_specs = P(("groups", "rep"), "tp")
    body = functools.partial(local, mesh.shape["tp"], mesh.shape["rep"])
    return jax.shard_map(body, mesh=mesh, in_specs=in_specs, out_specs=out_specs, check_vma=False)
```

```python
import functools

import jax
import jax.numpy as jnp
from jax import lax
from jax.experimental import pallas as pl
from jax.experimental.pallas import tpu as pltpu
from jax.sharding import PartitionSpec as P

MESH = pl.DeviceIdType.MESH


def kernel(
    geo, variants_ref, homes_ref, scale_ref, tok_ref, base_ref, code_ref, out_ref,
    variant_ref, home_ref, tok_buf, code_buf, base_buf, scale_buf, scale_full, total,
    tok_send, tok_recv, code_send, code_recv, scale_send, scale_recv, local_sem,
):
    tps, reps, tok_parts, code_parts, slots, block, width = geo
    chips = reps // 2
    rep = lax.axis_index("rep")
    tp = lax.axis_index("tp")
    core = lax.rem(rep, 2)
    chip = rep // 2
    partner = {"rep": rep + 1 - 2 * core}
    depth = tok_ref.shape[1]
    code_step = slots // code_parts

    own = [
        pltpu.make_async_copy(code_ref, code_buf.at[pl.ds(rep * slots, slots)], local_sem.at[0]),
        pltpu.make_async_copy(tok_ref, tok_buf.at[tp], local_sem.at[1]),
        pltpu.make_async_copy(base_ref, base_buf, local_sem.at[2]),
        pltpu.make_async_copy(scale_ref, scale_buf.at[rep], local_sem.at[3]),
        pltpu.make_async_copy(variants_ref, variant_ref, local_sem.at[4]),
        pltpu.make_async_copy(homes_ref, home_ref, local_sem.at[5]),
    ]

    barrier = pltpu.get_barrier_semaphore()

    def greet(device):
        pl.semaphore_signal(barrier, inc=1, device_id=device, device_id_type=MESH)

    greet(partner)
    sides = []
    for axis, me, place, stride, count in (("tp", tp, tp, 1, tps), ("rep", rep, chip, 2, chips)):
        up = (place < count - 1, {axis: me + stride})
        down = (place > 0, {axis: me - stride})
        for there, device in (up, down):
            pl.when(there)(functools.partial(greet, device))
        sides.append((up, down))
    (tok_up, tok_down), (code_up, code_down) = sides
    met = 1 + sum(there.astype(jnp.int32) for there, _ in (tok_up, tok_down, code_up, code_down))
    pl.semaphore_wait(barrier, met)

    def tok_copy(src, owner, part, way, hop, device):
        cols = pl.ds(*tok_parts[part])
        return pltpu.make_async_remote_copy(
            src_ref=tok_ref.at[:, cols] if src is None else tok_buf.at[owner, :, cols],
            dst_ref=tok_buf.at[owner, :, cols],
            send_sem=tok_send.at[way, hop, part],
            recv_sem=tok_recv.at[owner, part],
            device_id=device,
            device_id_type=MESH,
        )

    def code_copy(src, owner, part, way, hop, device):
        rows = pl.ds(owner * slots + part * code_step, code_step)
        return pltpu.make_async_remote_copy(
            src_ref=code_ref.at[pl.ds(part * code_step, code_step)] if src is None else code_buf.at[rows],
            dst_ref=code_buf.at[rows],
            send_sem=code_send.at[way, hop, part],
            recv_sem=code_recv.at[owner, part],
            device_id=device,
            device_id_type=MESH,
        )

    def scale_copy(src, owner, way, hop, device):
        return pltpu.make_async_remote_copy(
            src_ref=scale_ref if src is None else scale_buf.at[owner],
            dst_ref=scale_buf.at[owner],
            send_sem=scale_send.at[way, hop],
            recv_sem=scale_recv.at[owner],
            device_id=device,
            device_id_type=MESH,
        )

    for way, (there, device) in enumerate((tok_up, tok_down)):
        @pl.when(there)
        def _():
            for part in range(len(tok_parts)):
                tok_copy(None, tp, part, way, 0, device).start()

    for way, (there, device) in enumerate((code_up, code_down)):
        @pl.when(there)
        def _():
            scale_copy(None, rep, way, 0, device).start()
            for part in range(code_parts):
                code_copy(None, rep, part, way, 0, device).start()

    scale_copy(None, rep, 2, 0, partner).start()
    for part in range(code_parts):
        code_copy(None, rep, part, 2, 0, partner).start()
    for copy in own:
        copy.start()

    events = [
        ((hop * depth + sum(tok_parts[part])) * tok_ref.shape[0], 0, hop, part)
        for hop in range(tps - 2) for part in range(len(tok_parts))
    ] + [
        ((hop * code_parts + part + 1) * code_step * block * width, 1, hop, part)
        for hop in range(chips - 1) for part in range(code_parts)
    ]
    for _, kind, hop, part in sorted(events):
        for way in range(2):
            sign = 1 - 2 * way
            if kind == 0:
                place, count = tp, tps
                origin = tp - sign * (hop + 1)
                owner = origin
                onward = (tok_up, tok_down)[way]
            else:
                place, count = chip, chips
                origin = chip - sign * (hop + 1)
                owner = rep - 2 * sign * (hop + 1)
                onward = (code_up, code_down)[way]

            @pl.when((origin >= 0) & (origin < count))
            def _():
                if kind == 0:
                    tok_copy(1, owner, part, way, 0, partner).wait_recv()
                    @pl.when(onward[0])
                    def _():
                        tok_copy(1, owner, part, way, hop + 1, onward[1]).start()
                else:
                    if part == 0:
                        scale_copy(1, owner, way, 0, partner).wait_recv()
                    code_copy(1, owner, part, way, 0, partner).wait_recv()
                    if part == 0:
                        scale_copy(1, owner, 2 + way, hop + 1, partner).start()
                    code_copy(1, owner, part, 2 + way, hop + 1, partner).start()
                    if hop < chips - 2:
                        @pl.when(onward[0])
                        def _():
                            if part == 0:
                                scale_copy(1, owner, way, hop + 1, onward[1]).start()
                            code_copy(1, owner, part, way, hop + 1, onward[1]).start()

    for other in range(chips):
        owner = 2 * other + 1 - core
        scale_copy(1, owner, 0, 0, partner).wait_recv()
        for part in range(code_parts):
            code_copy(1, owner, part, 0, 0, partner).wait_recv()
    for copy in own:
        copy.wait()

    slot_row = lax.broadcasted_iota(jnp.int32, (slots, slots), 0)
    diagonal = slot_row == lax.broadcasted_iota(jnp.int32, (slots, slots), 1)
    for owner in range(reps):
        scales = scale_buf[owner].astype(jnp.float32)
        for col in range(scales.shape[0]):
            across = jnp.broadcast_to(scales[col:col + 1, :], (slots, slots))
            down = jnp.sum(jnp.where(diagonal, across, 0.0), axis=1, keepdims=True)
            scale_full[owner * slots:(owner + 1) * slots, col * block:(col + 1) * block] = (
                jnp.broadcast_to(down, (slots, block))
            )

    variant = variant_ref[rep]
    rows = tok_ref.shape[0]
    group = 4
    span = group * block

    def merge_and_multiply(first, shards):
        here = pl.ds(0, shards * rows)
        total[here, :] = jnp.zeros((shards * rows, width), jnp.float32)

        def step(at, carry):
            merged = []
            for i in range(group):
                b = at * group + i
                e = home_ref[variant, b]
                delta = code_buf[e].astype(jnp.float32) * scale_full[pl.ds(e, 1), :]
                lines = pl.ds(pl.multiple_of(b * block, block), block)
                merged.append((base_buf[lines, :].astype(jnp.float32) + delta).astype(jnp.bfloat16))
            merged = jnp.concatenate(merged, axis=0)
            cols = pl.ds(pl.multiple_of(at * span, span), span)
            if shards < tps:
                base_buf[cols, :] = merged
            prompt = tok_buf[pl.ds(first, shards), :, cols].reshape(shards * rows, span)
            total[here, :] += jnp.dot(prompt, merged, preferred_element_type=jnp.float32)
            return carry

        lax.fori_loop(0, depth // span, step, 0)
        out_ref[pl.ds(pl.multiple_of(first * rows, rows), shards * rows), :] = total[here, :].astype(out_ref.dtype)

    at_end = (tp == 0) | (tp == tps - 1)

    @pl.when(at_end)
    def _():
        merge_and_multiply((tp > 0).astype(jnp.int32), tps - 1)
        far = tps - 1 - tp
        last = pl.ds(0, rows)
        total[last, :] = jnp.zeros((rows, width), jnp.float32)
        for part in range(len(tok_parts)):
            tok_copy(1, far, part, 0, 0, partner).wait_recv()

            def step(at, carry):
                cols = pl.ds(pl.multiple_of(tok_parts[part][0] + at * span, span), span)
                total[last, :] += jnp.dot(tok_buf[far, :, cols], base_buf[cols, :], preferred_element_type=jnp.float32)
                return carry

            lax.fori_loop(0, tok_parts[part][1] // span, step, 0)
        out_ref[pl.ds(pl.multiple_of(far * rows, rows), rows), :] = total[last, :].astype(out_ref.dtype)

    @pl.when(jnp.logical_not(at_end))
    def _():
        merge_and_multiply(0, tps)

    for way, (there, device) in enumerate((tok_up, tok_down)):
        for hop in range(tps - 1):
            origin = tp - (1 - 2 * way) * hop

            @pl.when(there & (origin >= 0) & (origin < tps))
            def _():
                for part in range(len(tok_parts)):
                    tok_copy(1, origin, part, way, hop, device).wait_send()
    for way, (there, device) in enumerate((code_up, code_down)):
        sign = 1 - 2 * way
        for hop in range(chips):
            origin = chip - sign * hop
            owner = rep - 2 * sign * hop
            here = (origin >= 0) & (origin < chips)
            if hop < chips - 1:
                @pl.when(there & here)
                def _():
                    scale_copy(1, owner, way, hop, device).wait_send()
                    for part in range(code_parts):
                        code_copy(1, owner, part, way, hop, device).wait_send()
            if hop or not way:
                @pl.when(here)
                def _():
                    scale_copy(1, owner, 2 + way, hop, partner).wait_send()
                    for part in range(code_parts):
                        code_copy(1, owner, part, 2 + way, hop, partner).wait_send()


def local(tps, reps, tokens, base_weight, delta_codes, delta_scales, replica_variant, block_home):
    slots, col_blocks = delta_scales.shape
    rows, depth = tokens.shape
    width = base_weight.shape[1]
    block = delta_codes.shape[0] // slots
    sizes = (depth // 2, depth // 4, depth // 8, depth // 8)
    tok_parts = tuple((sum(sizes[:i]), size) for i, size in enumerate(sizes))
    code_parts = max(1, 32 // reps)
    codes = delta_codes.reshape(slots, block, width)
    dma = pltpu.SemaphoreType.DMA
    chips = reps // 2
    return pl.pallas_call(
        functools.partial(kernel, (tps, reps, tok_parts, code_parts, slots, block, width)),
        out_shape=jax.ShapeDtypeStruct((tps * rows, width), jnp.bfloat16),
        in_specs=[pl.BlockSpec(memory_space=pl.ANY)] * 6,
        out_specs=pl.BlockSpec(memory_space=pltpu.VMEM),
        scratch_shapes=[
            pltpu.SMEM(replica_variant.shape, jnp.int32),
            pltpu.SMEM(block_home.shape, jnp.int32),
            pltpu.VMEM((tps, rows, depth), jnp.bfloat16),
            pltpu.VMEM((reps * slots, block, width), jnp.bfloat16),
            pltpu.VMEM((depth, width), jnp.bfloat16),
            pltpu.VMEM((reps, col_blocks, slots), jnp.bfloat16),
            pltpu.VMEM((reps * slots, width), jnp.float32),
            pltpu.VMEM((tps * rows, width), jnp.float32),
            dma((2, tps, len(tok_parts))),
            dma((tps, len(tok_parts))),
            dma((4, chips, code_parts)),
            dma((reps, code_parts)),
            dma((4, chips)),
            dma((reps,)),
            dma((6,)),
        ],
        compiler_params=pltpu.CompilerParams(
            collective_id=0, has_side_effects=True, vmem_limit_bytes=60 * 1024 * 1024
        ),
    )(replica_variant, block_home, delta_scales.T, tokens, base_weight, codes)


def solution(mesh):
    in_specs = (
        P(("groups", "rep", "tp"), None),
        P(None, "tp"),
        P(("groups", "rep"), "tp"),
        P(("groups", "rep"), "tp"),
        P("groups"),
        P("groups", None),
    )
    out_specs = P(("groups", "rep"), "tp")
    body = functools.partial(local, mesh.shape["tp"], mesh.shape["rep"])
    return jax.shard_map(body, mesh=mesh, in_specs=in_specs, out_specs=out_specs, check_vma=False)
```

```python
import functools

import jax
import jax.numpy as jnp
from jax import lax
from jax.experimental import pallas as pl
from jax.experimental.pallas import tpu as pltpu
from jax.sharding import PartitionSpec as P

MESH = pl.DeviceIdType.MESH


def kernel(
    geo, variants_ref, homes_ref, scale_ref, tok_ref, base_ref, code_ref, out_ref,
    variant_ref, home_ref, tok_buf, code_buf, base_buf, scale_buf, scale_full, total,
    tok_send, tok_recv, code_send, code_recv, scale_send, scale_recv, local_sem,
):
    tps, reps, tok_parts, code_parts, slots, block, width = geo
    chips = reps // 2
    rep = lax.axis_index("rep")
    tp = lax.axis_index("tp")
    core = lax.rem(rep, 2)
    chip = rep // 2
    partner = {"rep": rep + 1 - 2 * core}
    depth = tok_ref.shape[1]
    code_step = slots // code_parts

    own = [
        pltpu.make_async_copy(code_ref, code_buf.at[pl.ds(rep * slots, slots)], local_sem.at[0]),
        pltpu.make_async_copy(tok_ref, tok_buf.at[tp], local_sem.at[1]),
        pltpu.make_async_copy(base_ref, base_buf, local_sem.at[2]),
        pltpu.make_async_copy(scale_ref, scale_buf.at[rep], local_sem.at[3]),
        pltpu.make_async_copy(variants_ref, variant_ref, local_sem.at[4]),
        pltpu.make_async_copy(homes_ref, home_ref, local_sem.at[5]),
    ]

    barrier = pltpu.get_barrier_semaphore()

    def greet(device):
        pl.semaphore_signal(barrier, inc=1, device_id=device, device_id_type=MESH)

    greet(partner)
    sides = []
    for axis, me, place, stride, count in (("tp", tp, tp, 1, tps), ("rep", rep, chip, 2, chips)):
        up = (place < count - 1, {axis: me + stride})
        down = (place > 0, {axis: me - stride})
        for there, device in (up, down):
            pl.when(there)(functools.partial(greet, device))
        sides.append((up, down))
    (tok_up, tok_down), (code_up, code_down) = sides
    met = 1 + sum(there.astype(jnp.int32) for there, _ in (tok_up, tok_down, code_up, code_down))
    pl.semaphore_wait(barrier, met)

    def tok_copy(src, owner, part, way, hop, device):
        cols = pl.ds(*tok_parts[part])
        return pltpu.make_async_remote_copy(
            src_ref=tok_ref.at[:, cols] if src is None else tok_buf.at[owner, :, cols],
            dst_ref=tok_buf.at[owner, :, cols],
            send_sem=tok_send.at[way, hop, part],
            recv_sem=tok_recv.at[owner, part],
            device_id=device,
            device_id_type=MESH,
        )

    def code_copy(src, owner, part, way, hop, device):
        rows = pl.ds(owner * slots + part * code_step, code_step)
        return pltpu.make_async_remote_copy(
            src_ref=code_ref.at[pl.ds(part * code_step, code_step)] if src is None else code_buf.at[rows],
            dst_ref=code_buf.at[rows],
            send_sem=code_send.at[way, hop, part],
            recv_sem=code_recv.at[owner, part],
            device_id=device,
            device_id_type=MESH,
        )

    def scale_copy(src, owner, way, hop, device):
        return pltpu.make_async_remote_copy(
            src_ref=scale_ref if src is None else scale_buf.at[owner],
            dst_ref=scale_buf.at[owner],
            send_sem=scale_send.at[way, hop],
            recv_sem=scale_recv.at[owner],
            device_id=device,
            device_id_type=MESH,
        )

    for way, (there, device) in enumerate((tok_up, tok_down)):
        @pl.when(there)
        def _():
            for part in range(len(tok_parts)):
                tok_copy(None, tp, part, way, 0, device).start()

    for way, (there, device) in enumerate((code_up, code_down)):
        @pl.when(there)
        def _():
            scale_copy(None, rep, way, 0, device).start()
            for part in range(code_parts):
                code_copy(None, rep, part, way, 0, device).start()

    scale_copy(None, rep, 2, 0, partner).start()
    for part in range(code_parts):
        code_copy(None, rep, part, 2, 0, partner).start()
    for copy in own:
        copy.start()

    events = [
        ((hop * depth + sum(tok_parts[part])) * tok_ref.shape[0], 0, hop, part)
        for hop in range(tps - 2) for part in range(len(tok_parts))
    ] + [
        ((hop * code_parts + part + 1) * code_step * block * width, 1, hop, part)
        for hop in range(chips - 1) for part in range(code_parts)
    ]
    for _, kind, hop, part in sorted(events):
        for way in range(2):
            sign = 1 - 2 * way
            if kind == 0:
                place, count = tp, tps
                origin = tp - sign * (hop + 1)
                owner = origin
                onward = (tok_up, tok_down)[way]
            else:
                place, count = chip, chips
                origin = chip - sign * (hop + 1)
                owner = rep - 2 * sign * (hop + 1)
                onward = (code_up, code_down)[way]

            @pl.when((origin >= 0) & (origin < count))
            def _():
                if kind == 0:
                    tok_copy(1, owner, part, way, 0, partner).wait_recv()
                    @pl.when(onward[0])
                    def _():
                        tok_copy(1, owner, part, way, hop + 1, onward[1]).start()
                else:
                    if part == 0:
                        scale_copy(1, owner, way, 0, partner).wait_recv()
                    code_copy(1, owner, part, way, 0, partner).wait_recv()
                    if part == 0:
                        scale_copy(1, owner, 2 + way, hop + 1, partner).start()
                    code_copy(1, owner, part, 2 + way, hop + 1, partner).start()
                    if hop < chips - 2:
                        @pl.when(onward[0])
                        def _():
                            if part == 0:
                                scale_copy(1, owner, way, hop + 1, onward[1]).start()
                            code_copy(1, owner, part, way, hop + 1, onward[1]).start()

    for other in range(chips):
        owner = 2 * other + 1 - core
        scale_copy(1, owner, 0, 0, partner).wait_recv()
        for part in range(code_parts):
            code_copy(1, owner, part, 0, 0, partner).wait_recv()
    for copy in own:
        copy.wait()

    slot_row = lax.broadcasted_iota(jnp.int32, (slots, slots), 0)
    diagonal = slot_row == lax.broadcasted_iota(jnp.int32, (slots, slots), 1)
    for owner in range(reps):
        scales = scale_buf[owner].astype(jnp.float32)
        for col in range(scales.shape[0]):
            across = jnp.broadcast_to(scales[col:col + 1, :], (slots, slots))
            down = jnp.sum(jnp.where(diagonal, across, 0.0), axis=1, keepdims=True)
            scale_full[owner * slots:(owner + 1) * slots, col * block:(col + 1) * block] = (
                jnp.broadcast_to(down, (slots, block))
            )

    variant = variant_ref[rep]
    rows = tok_ref.shape[0]
    group = 8
    span = group * block

    def merge_and_multiply(first, shards):
        here = pl.ds(0, shards * rows)
        total[here, :] = jnp.zeros((shards * rows, width), jnp.float32)

        def step(at, carry):
            merged = []
            for i in range(group):
                b = at * group + i
                e = home_ref[variant, b]
                delta = code_buf[e].astype(jnp.float32) * scale_full[pl.ds(e, 1), :]
                lines = pl.ds(pl.multiple_of(b * block, block), block)
                merged.append((base_buf[lines, :].astype(jnp.float32) + delta).astype(jnp.bfloat16))
            merged = jnp.concatenate(merged, axis=0)
            cols = pl.ds(pl.multiple_of(at * span, span), span)
            if shards < tps:
                base_buf[cols, :] = merged
            prompt = tok_buf[pl.ds(first, shards), :, cols].reshape(shards * rows, span)
            total[here, :] += jnp.dot(prompt, merged, preferred_element_type=jnp.float32)
            return carry

        lax.fori_loop(0, depth // span, step, 0)
        out_ref[pl.ds(pl.multiple_of(first * rows, rows), shards * rows), :] = total[here, :].astype(out_ref.dtype)

    at_end = (tp == 0) | (tp == tps - 1)

    @pl.when(at_end)
    def _():
        merge_and_multiply((tp > 0).astype(jnp.int32), tps - 1)
        far = tps - 1 - tp
        last = pl.ds(0, rows)
        total[last, :] = jnp.zeros((rows, width), jnp.float32)
        for part in range(len(tok_parts)):
            tok_copy(1, far, part, 0, 0, partner).wait_recv()

            def step(at, carry):
                cols = pl.ds(pl.multiple_of(tok_parts[part][0] + at * span, span), span)
                total[last, :] += jnp.dot(tok_buf[far, :, cols], base_buf[cols, :], preferred_element_type=jnp.float32)
                return carry

            lax.fori_loop(0, tok_parts[part][1] // span, step, 0)
        out_ref[pl.ds(pl.multiple_of(far * rows, rows), rows), :] = total[last, :].astype(out_ref.dtype)

    @pl.when(jnp.logical_not(at_end))
    def _():
        merge_and_multiply(0, tps)

    for way, (there, device) in enumerate((tok_up, tok_down)):
        for hop in range(tps - 1):
            origin = tp - (1 - 2 * way) * hop

            @pl.when(there & (origin >= 0) & (origin < tps))
            def _():
                for part in range(len(tok_parts)):
                    tok_copy(1, origin, part, way, hop, device).wait_send()
    for way, (there, device) in enumerate((code_up, code_down)):
        sign = 1 - 2 * way
        for hop in range(chips):
            origin = chip - sign * hop
            owner = rep - 2 * sign * hop
            here = (origin >= 0) & (origin < chips)
            if hop < chips - 1:
                @pl.when(there & here)
                def _():
                    scale_copy(1, owner, way, hop, device).wait_send()
                    for part in range(code_parts):
                        code_copy(1, owner, part, way, hop, device).wait_send()
            if hop or not way:
                @pl.when(here)
                def _():
                    scale_copy(1, owner, 2 + way, hop, partner).wait_send()
                    for part in range(code_parts):
                        code_copy(1, owner, part, 2 + way, hop, partner).wait_send()


def local(tps, reps, tokens, base_weight, delta_codes, delta_scales, replica_variant, block_home):
    slots, col_blocks = delta_scales.shape
    rows, depth = tokens.shape
    width = base_weight.shape[1]
    block = delta_codes.shape[0] // slots
    sizes = (depth // 2, depth // 4, depth // 8, depth // 8)
    tok_parts = tuple((sum(sizes[:i]), size) for i, size in enumerate(sizes))
    code_parts = max(1, 32 // reps)
    codes = delta_codes.reshape(slots, block, width)
    operands = [
        pltpu.with_memory_space_constraint(x, pltpu.HBM)
        for x in (replica_variant, block_home, delta_scales.T, tokens, base_weight, codes)
    ]
    dma = pltpu.SemaphoreType.DMA
    chips = reps // 2
    return pl.pallas_call(
        functools.partial(kernel, (tps, reps, tok_parts, code_parts, slots, block, width)),
        out_shape=jax.ShapeDtypeStruct((tps * rows, width), jnp.bfloat16),
        in_specs=[pl.BlockSpec(memory_space=pl.ANY)] * 6,
        out_specs=pl.BlockSpec(memory_space=pltpu.VMEM),
        scratch_shapes=[
            pltpu.SMEM(replica_variant.shape, jnp.int32),
            pltpu.SMEM(block_home.shape, jnp.int32),
            pltpu.VMEM((tps, rows, depth), jnp.bfloat16),
            pltpu.VMEM((reps * slots, block, width), jnp.bfloat16),
            pltpu.VMEM((depth, width), jnp.bfloat16),
            pltpu.VMEM((reps, col_blocks, slots), jnp.bfloat16),
            pltpu.VMEM((reps * slots, width), jnp.float32),
            pltpu.VMEM((tps * rows, width), jnp.float32),
            dma((2, tps, len(tok_parts))),
            dma((tps, len(tok_parts))),
            dma((4, chips, code_parts)),
            dma((reps, code_parts)),
            dma((4, chips)),
            dma((reps,)),
            dma((6,)),
        ],
        compiler_params=pltpu.CompilerParams(
            collective_id=0, has_side_effects=True, vmem_limit_bytes=54 * 1024 * 1024
        ),
    )(*operands)


def solution(mesh):
    in_specs = (
        P(("groups", "rep", "tp"), None),
        P(None, "tp"),
        P(("groups", "rep"), "tp"),
        P(("groups", "rep"), "tp"),
        P("groups"),
        P("groups", None),
    )
    out_specs = P(("groups", "rep"), "tp")
    body = functools.partial(local, mesh.shape["tp"], mesh.shape["rep"])
    return jax.shard_map(body, mesh=mesh, in_specs=in_specs, out_specs=out_specs, check_vma=False)
```

```python
import functools

import jax
import jax.numpy as jnp
from jax import lax
from jax.experimental import pallas as pl
from jax.experimental.pallas import tpu as pltpu
from jax.sharding import PartitionSpec as P

MESH = pl.DeviceIdType.MESH


def kernel(
    geo, variants_ref, homes_ref, scale_ref, tok_ref, base_ref, code_ref, out_ref,
    variant_ref, home_ref, tok_buf, code_buf, base_buf, scale_buf, scale_full, total,
    tok_send, tok_recv, code_send, code_recv, scale_send, scale_recv, local_sem,
):
    tps, reps, tok_parts, code_parts, slots, block, width = geo
    chips = reps // 2
    rep = lax.axis_index("rep")
    tp = lax.axis_index("tp")
    core = lax.rem(rep, 2)
    chip = rep // 2
    partner = {"rep": rep + 1 - 2 * core}
    depth = tok_ref.shape[1]
    code_step = slots // code_parts

    own = [
        pltpu.make_async_copy(code_ref, code_buf.at[pl.ds(rep * slots, slots)], local_sem.at[0]),
        pltpu.make_async_copy(tok_ref, tok_buf.at[tp], local_sem.at[1]),
        pltpu.make_async_copy(base_ref, base_buf, local_sem.at[2]),
        pltpu.make_async_copy(scale_ref, scale_buf.at[rep], local_sem.at[3]),
        pltpu.make_async_copy(variants_ref, variant_ref, local_sem.at[4]),
        pltpu.make_async_copy(homes_ref, home_ref, local_sem.at[5]),
    ]

    barrier = pltpu.get_barrier_semaphore()

    def greet(device):
        pl.semaphore_signal(barrier, inc=1, device_id=device, device_id_type=MESH)

    greet(partner)
    sides = []
    for axis, me, place, stride, count in (("tp", tp, tp, 1, tps), ("rep", rep, chip, 2, chips)):
        up = (place < count - 1, {axis: me + stride})
        down = (place > 0, {axis: me - stride})
        for there, device in (up, down):
            pl.when(there)(functools.partial(greet, device))
        sides.append((up, down))
    (tok_up, tok_down), (code_up, code_down) = sides
    met = 1 + sum(there.astype(jnp.int32) for there, _ in (tok_up, tok_down, code_up, code_down))
    pl.semaphore_wait(barrier, met)

    def tok_copy(src, owner, part, way, hop, device):
        cols = pl.ds(*tok_parts[part])
        return pltpu.make_async_remote_copy(
            src_ref=tok_ref.at[:, cols] if src is None else tok_buf.at[owner, :, cols],
            dst_ref=tok_buf.at[owner, :, cols],
            send_sem=tok_send.at[way, hop, part],
            recv_sem=tok_recv.at[owner, part],
            device_id=device,
            device_id_type=MESH,
        )

    def code_copy(src, owner, part, way, hop, device):
        rows = pl.ds(owner * slots + part * code_step, code_step)
        return pltpu.make_async_remote_copy(
            src_ref=code_ref.at[pl.ds(part * code_step, code_step)] if src is None else code_buf.at[rows],
            dst_ref=code_buf.at[rows],
            send_sem=code_send.at[way, hop, part],
            recv_sem=code_recv.at[owner, part],
            device_id=device,
            device_id_type=MESH,
        )

    def scale_copy(src, owner, way, hop, device):
        return pltpu.make_async_remote_copy(
            src_ref=scale_ref if src is None else scale_buf.at[owner],
            dst_ref=scale_buf.at[owner],
            send_sem=scale_send.at[way, hop],
            recv_sem=scale_recv.at[owner],
            device_id=device,
            device_id_type=MESH,
        )

    for way, (there, device) in enumerate((tok_up, tok_down)):
        @pl.when(there)
        def _():
            for part in range(len(tok_parts)):
                tok_copy(None, tp, part, way, 0, device).start()

    for way, (there, device) in enumerate((code_up, code_down)):
        @pl.when(there)
        def _():
            scale_copy(None, rep, way, 0, device).start()
            for part in range(code_parts):
                code_copy(None, rep, part, way, 0, device).start()

    scale_copy(None, rep, 2, 0, partner).start()
    for part in range(code_parts):
        code_copy(None, rep, part, 2, 0, partner).start()
    for copy in own:
        copy.start()

    events = [
        ((hop * depth + sum(tok_parts[part])) * tok_ref.shape[0], 0, hop, part)
        for hop in range(tps - 2) for part in range(len(tok_parts))
    ] + [
        ((hop * code_parts + part + 1) * code_step * block * width, 1, hop, part)
        for hop in range(chips - 1) for part in range(code_parts)
    ]
    for _, kind, hop, part in sorted(events):
        for way in range(2):
            sign = 1 - 2 * way
            if kind == 0:
                place, count = tp, tps
                origin = tp - sign * (hop + 1)
                owner = origin
                onward = (tok_up, tok_down)[way]
            else:
                place, count = chip, chips
                origin = chip - sign * (hop + 1)
                owner = rep - 2 * sign * (hop + 1)
                onward = (code_up, code_down)[way]

            @pl.when((origin >= 0) & (origin < count))
            def _():
                if kind == 0:
                    tok_copy(1, owner, part, way, 0, partner).wait_recv()
                    @pl.when(onward[0])
                    def _():
                        tok_copy(1, owner, part, way, hop + 1, onward[1]).start()
                else:
                    if part == 0:
                        scale_copy(1, owner, way, 0, partner).wait_recv()
                    code_copy(1, owner, part, way, 0, partner).wait_recv()
                    if part == 0:
                        scale_copy(1, owner, 2 + way, hop + 1, partner).start()
                    code_copy(1, owner, part, 2 + way, hop + 1, partner).start()
                    if hop < chips - 2:
                        @pl.when(onward[0])
                        def _():
                            if part == 0:
                                scale_copy(1, owner, way, hop + 1, onward[1]).start()
                            code_copy(1, owner, part, way, hop + 1, onward[1]).start()

    for other in range(chips):
        owner = 2 * other + 1 - core
        scale_copy(1, owner, 0, 0, partner).wait_recv()
        for part in range(code_parts):
            code_copy(1, owner, part, 0, 0, partner).wait_recv()
    for copy in own:
        copy.wait()

    slot_row = lax.broadcasted_iota(jnp.int32, (slots, slots), 0)
    diagonal = slot_row == lax.broadcasted_iota(jnp.int32, (slots, slots), 1)
    for owner in range(reps):
        scales = scale_buf[owner].astype(jnp.float32)
        for col in range(scales.shape[0]):
            across = jnp.broadcast_to(scales[col:col + 1, :], (slots, slots))
            down = jnp.sum(jnp.where(diagonal, across, 0.0), axis=1, keepdims=True)
            scale_full[owner * slots:(owner + 1) * slots, col * block:(col + 1) * block] = (
                jnp.broadcast_to(down, (slots, block))
            )

    variant = variant_ref[rep]
    rows = tok_ref.shape[0]
    group = 8
    span = group * block

    def merge_and_multiply(first, shards):
        here = pl.ds(0, shards * rows)
        total[here, :] = jnp.zeros((shards * rows, width), jnp.float32)

        def step(at, carry):
            merged = []
            for i in range(group):
                b = at * group + i
                e = home_ref[variant, b]
                delta = code_buf[e].astype(jnp.float32) * scale_full[pl.ds(e, 1), :]
                lines = pl.ds(pl.multiple_of(b * block, block), block)
                merged.append((base_buf[lines, :].astype(jnp.float32) + delta).astype(jnp.bfloat16))
            merged = jnp.concatenate(merged, axis=0)
            cols = pl.ds(pl.multiple_of(at * span, span), span)
            if shards < tps:
                base_buf[cols, :] = merged
            prompt = tok_buf[pl.ds(first, shards), :, cols].reshape(shards * rows, span)
            total[here, :] += jnp.dot(prompt, merged, preferred_element_type=jnp.float32)
            return carry

        lax.fori_loop(0, depth // span, step, 0)
        out_ref[pl.ds(pl.multiple_of(first * rows, rows), shards * rows), :] = total[here, :].astype(out_ref.dtype)

    at_end = (tp == 0) | (tp == tps - 1)

    @pl.when(at_end)
    def _():
        merge_and_multiply((tp > 0).astype(jnp.int32), tps - 1)
        far = tps - 1 - tp
        last = pl.ds(0, rows)
        total[last, :] = jnp.zeros((rows, width), jnp.float32)
        for part in range(len(tok_parts)):
            tok_copy(1, far, part, 0, 0, partner).wait_recv()

            def step(at, carry):
                cols = pl.ds(pl.multiple_of(tok_parts[part][0] + at * span, span), span)
                total[last, :] += jnp.dot(tok_buf[far, :, cols], base_buf[cols, :], preferred_element_type=jnp.float32)
                return carry

            lax.fori_loop(0, tok_parts[part][1] // span, step, 0)
        out_ref[pl.ds(pl.multiple_of(far * rows, rows), rows), :] = total[last, :].astype(out_ref.dtype)

    @pl.when(jnp.logical_not(at_end))
    def _():
        merge_and_multiply(0, tps)

    for way, (there, device) in enumerate((tok_up, tok_down)):
        for hop in range(tps - 1):
            origin = tp - (1 - 2 * way) * hop

            @pl.when(there & (origin >= 0) & (origin < tps))
            def _():
                for part in range(len(tok_parts)):
                    tok_copy(1, origin, part, way, hop, device).wait_send()
    for way, (there, device) in enumerate((code_up, code_down)):
        sign = 1 - 2 * way
        for hop in range(chips):
            origin = chip - sign * hop
            owner = rep - 2 * sign * hop
            here = (origin >= 0) & (origin < chips)
            if hop < chips - 1:
                @pl.when(there & here)
                def _():
                    scale_copy(1, owner, way, hop, device).wait_send()
                    for part in range(code_parts):
                        code_copy(1, owner, part, way, hop, device).wait_send()
            if hop or not way:
                @pl.when(here)
                def _():
                    scale_copy(1, owner, 2 + way, hop, partner).wait_send()
                    for part in range(code_parts):
                        code_copy(1, owner, part, 2 + way, hop, partner).wait_send()


def local(tps, reps, tokens, base_weight, delta_codes, delta_scales, replica_variant, block_home):
    slots, col_blocks = delta_scales.shape
    rows, depth = tokens.shape
    width = base_weight.shape[1]
    block = delta_codes.shape[0] // slots
    sizes = (depth // 2, depth // 4, depth // 8, depth // 8)
    tok_parts = tuple((sum(sizes[:i]), size) for i, size in enumerate(sizes))
    code_parts = max(1, 8 // reps)
    codes = delta_codes.reshape(slots, block, width)
    operands = [
        pltpu.with_memory_space_constraint(x, pltpu.HBM)
        for x in (replica_variant, block_home, delta_scales.T, tokens, base_weight, codes)
    ]
    dma = pltpu.SemaphoreType.DMA
    chips = reps // 2
    return pl.pallas_call(
        functools.partial(kernel, (tps, reps, tok_parts, code_parts, slots, block, width)),
        out_shape=jax.ShapeDtypeStruct((tps * rows, width), jnp.bfloat16),
        in_specs=[pl.BlockSpec(memory_space=pl.ANY)] * 6,
        out_specs=pl.BlockSpec(memory_space=pltpu.VMEM),
        scratch_shapes=[
            pltpu.SMEM(replica_variant.shape, jnp.int32),
            pltpu.SMEM(block_home.shape, jnp.int32),
            pltpu.VMEM((tps, rows, depth), jnp.bfloat16),
            pltpu.VMEM((reps * slots, block, width), jnp.bfloat16),
            pltpu.VMEM((depth, width), jnp.bfloat16),
            pltpu.VMEM((reps, col_blocks, slots), jnp.bfloat16),
            pltpu.VMEM((reps * slots, width), jnp.float32),
            pltpu.VMEM((tps * rows, width), jnp.float32),
            dma((2, tps, len(tok_parts))),
            dma((tps, len(tok_parts))),
            dma((4, chips, code_parts)),
            dma((reps, code_parts)),
            dma((4, chips)),
            dma((reps,)),
            dma((6,)),
        ],
        compiler_params=pltpu.CompilerParams(
            collective_id=0, has_side_effects=True, vmem_limit_bytes=48 * 1024 * 1024
        ),
    )(*operands)


def solution(mesh):
    in_specs = (
        P(("groups", "rep", "tp"), None),
        P(None, "tp"),
        P(("groups", "rep"), "tp"),
        P(("groups", "rep"), "tp"),
        P("groups"),
        P("groups", None),
    )
    out_specs = P(("groups", "rep"), "tp")
    body = functools.partial(local, mesh.shape["tp"], mesh.shape["rep"])
    return jax.shard_map(body, mesh=mesh, in_specs=in_specs, out_specs=out_specs, check_vma=False)
```

```python
import functools

import jax
import jax.numpy as jnp
from jax import lax
from jax.experimental import pallas as pl
from jax.experimental.pallas import tpu as pltpu
from jax.sharding import PartitionSpec as P

MESH = pl.DeviceIdType.MESH


def kernel(
    geo, variants_ref, homes_ref, scale_ref, tok_ref, base_ref, code_ref, out_ref,
    variant_ref, home_ref, tok_buf, code_buf, base_buf, scale_buf, scale_full, total,
    tok_send, tok_recv, code_send, code_recv, scale_send, scale_recv, local_sem,
):
    tps, reps, tok_parts, code_parts, slots, block, width = geo
    chips = reps // 2
    rep = lax.axis_index("rep")
    tp = lax.axis_index("tp")
    core = lax.rem(rep, 2)
    chip = rep // 2
    partner = {"rep": rep + 1 - 2 * core}
    depth = tok_ref.shape[1]
    code_step = slots // code_parts

    own = [
        pltpu.make_async_copy(code_ref, code_buf.at[pl.ds(rep * slots, slots)], local_sem.at[0]),
        pltpu.make_async_copy(tok_ref, tok_buf.at[tp], local_sem.at[1]),
        pltpu.make_async_copy(base_ref, base_buf, local_sem.at[2]),
        pltpu.make_async_copy(scale_ref, scale_buf.at[rep], local_sem.at[3]),
        pltpu.make_async_copy(variants_ref, variant_ref, local_sem.at[4]),
        pltpu.make_async_copy(homes_ref, home_ref, local_sem.at[5]),
    ]

    barrier = pltpu.get_barrier_semaphore()

    def greet(device):
        pl.semaphore_signal(barrier, inc=1, device_id=device, device_id_type=MESH)

    greet(partner)
    sides = []
    for axis, me, place, stride, count in (("tp", tp, tp, 1, tps), ("rep", rep, chip, 2, chips)):
        up = (place < count - 1, {axis: me + stride})
        down = (place > 0, {axis: me - stride})
        for there, device in (up, down):
            pl.when(there)(functools.partial(greet, device))
        sides.append((up, down))
    (tok_up, tok_down), (code_up, code_down) = sides
    met = 1 + sum(there.astype(jnp.int32) for there, _ in (tok_up, tok_down, code_up, code_down))
    pl.semaphore_wait(barrier, met)

    def tok_copy(src, owner, part, way, hop, device):
        cols = pl.ds(*tok_parts[part])
        return pltpu.make_async_remote_copy(
            src_ref=tok_ref.at[:, cols] if src is None else tok_buf.at[owner, :, cols],
            dst_ref=tok_buf.at[owner, :, cols],
            send_sem=tok_send.at[way, hop, part],
            recv_sem=tok_recv.at[owner, part],
            device_id=device,
            device_id_type=MESH,
        )

    def code_copy(src, owner, part, way, hop, device):
        rows = pl.ds(owner * slots + part * code_step, code_step)
        return pltpu.make_async_remote_copy(
            src_ref=code_ref.at[pl.ds(part * code_step, code_step)] if src is None else code_buf.at[rows],
            dst_ref=code_buf.at[rows],
            send_sem=code_send.at[way, hop, part],
            recv_sem=code_recv.at[owner, part],
            device_id=device,
            device_id_type=MESH,
        )

    def scale_copy(src, owner, way, hop, device):
        return pltpu.make_async_remote_copy(
            src_ref=scale_ref if src is None else scale_buf.at[owner],
            dst_ref=scale_buf.at[owner],
            send_sem=scale_send.at[way, hop],
            recv_sem=scale_recv.at[owner],
            device_id=device,
            device_id_type=MESH,
        )

    for way, (there, device) in enumerate((tok_up, tok_down)):
        @pl.when(there)
        def _():
            for part in range(len(tok_parts)):
                tok_copy(None, tp, part, way, 0, device).start()

    for way, (there, device) in enumerate((code_up, code_down)):
        @pl.when(there)
        def _():
            scale_copy(None, rep, way, 0, device).start()
            for part in range(code_parts):
                code_copy(None, rep, part, way, 0, device).start()

    scale_copy(None, rep, 2, 0, partner).start()
    for part in range(code_parts):
        code_copy(None, rep, part, 2, 0, partner).start()
    for copy in own:
        copy.start()

    events = [
        ((hop * depth + sum(tok_parts[part])) * tok_ref.shape[0], 0, hop, part)
        for hop in range(tps - 2) for part in range(len(tok_parts))
    ] + [
        ((hop * code_parts + part + 1) * code_step * block * width, 1, hop, part)
        for hop in range(chips - 1) for part in range(code_parts)
    ]
    for _, kind, hop, part in sorted(events):
        for way in range(2):
            sign = 1 - 2 * way
            if kind == 0:
                place, count = tp, tps
                origin = tp - sign * (hop + 1)
                owner = origin
                onward = (tok_up, tok_down)[way]
            else:
                place, count = chip, chips
                origin = chip - sign * (hop + 1)
                owner = rep - 2 * sign * (hop + 1)
                onward = (code_up, code_down)[way]

            @pl.when((origin >= 0) & (origin < count))
            def _():
                if kind == 0:
                    tok_copy(1, owner, part, way, 0, partner).wait_recv()
                    @pl.when(onward[0])
                    def _():
                        tok_copy(1, owner, part, way, hop + 1, onward[1]).start()
                else:
                    if part == 0:
                        scale_copy(1, owner, way, 0, partner).wait_recv()
                    code_copy(1, owner, part, way, 0, partner).wait_recv()
                    if part == 0:
                        scale_copy(1, owner, 2 + way, hop + 1, partner).start()
                    code_copy(1, owner, part, 2 + way, hop + 1, partner).start()
                    if hop < chips - 2:
                        @pl.when(onward[0])
                        def _():
                            if part == 0:
                                scale_copy(1, owner, way, hop + 1, onward[1]).start()
                            code_copy(1, owner, part, way, hop + 1, onward[1]).start()

    for other in range(chips):
        owner = 2 * other + 1 - core
        scale_copy(1, owner, 0, 0, partner).wait_recv()
        for part in range(code_parts):
            code_copy(1, owner, part, 0, 0, partner).wait_recv()
    for copy in own:
        copy.wait()

    slot_row = lax.broadcasted_iota(jnp.int32, (slots, slots), 0)
    diagonal = slot_row == lax.broadcasted_iota(jnp.int32, (slots, slots), 1)
    for owner in range(reps):
        scales = scale_buf[owner].astype(jnp.float32)
        for col in range(scales.shape[0]):
            across = jnp.broadcast_to(scales[col:col + 1, :], (slots, slots))
            down = jnp.sum(jnp.where(diagonal, across, 0.0), axis=1, keepdims=True)
            scale_full[owner * slots:(owner + 1) * slots, col * block:(col + 1) * block] = (
                jnp.broadcast_to(down, (slots, block))
            )

    variant = variant_ref[rep]
    rows = tok_ref.shape[0]
    group = 8
    span = group * block

    def merge_and_multiply(first, shards):
        here = pl.ds(0, shards * rows)
        total[here, :] = jnp.zeros((shards * rows, width), jnp.float32)

        def step(at, carry):
            merged = []
            for i in range(group):
                b = at * group + i
                e = home_ref[variant, b]
                delta = code_buf[e].astype(jnp.float32) * scale_full[pl.ds(e, 1), :]
                lines = pl.ds(pl.multiple_of(b * block, block), block)
                merged.append((base_buf[lines, :].astype(jnp.float32) + delta).astype(jnp.bfloat16))
            merged = jnp.concatenate(merged, axis=0)
            cols = pl.ds(pl.multiple_of(at * span, span), span)
            if shards < tps:
                base_buf[cols, :] = merged
            prompt = tok_buf[pl.ds(first, shards), :, cols].reshape(shards * rows, span)
            total[here, :] += jnp.dot(prompt, merged, preferred_element_type=jnp.float32)
            return carry

        lax.fori_loop(0, depth // span, step, 0)
        out_ref[pl.ds(pl.multiple_of(first * rows, rows), shards * rows), :] = total[here, :].astype(out_ref.dtype)

    at_end = (tp == 0) | (tp == tps - 1)

    @pl.when(at_end)
    def _():
        merge_and_multiply((tp > 0).astype(jnp.int32), tps - 1)
        far = tps - 1 - tp
        last = pl.ds(0, rows)
        total[last, :] = jnp.zeros((rows, width), jnp.float32)
        for part in range(len(tok_parts)):
            tok_copy(1, far, part, 0, 0, partner).wait_recv()

            def step(at, carry):
                cols = pl.ds(pl.multiple_of(tok_parts[part][0] + at * span, span), span)
                total[last, :] += jnp.dot(tok_buf[far, :, cols], base_buf[cols, :], preferred_element_type=jnp.float32)
                return carry

            lax.fori_loop(0, tok_parts[part][1] // span, step, 0)
        out_ref[pl.ds(pl.multiple_of(far * rows, rows), rows), :] = total[last, :].astype(out_ref.dtype)

    @pl.when(jnp.logical_not(at_end))
    def _():
        merge_and_multiply(0, tps)

    for way, (there, device) in enumerate((tok_up, tok_down)):
        for hop in range(tps - 1):
            origin = tp - (1 - 2 * way) * hop

            @pl.when(there & (origin >= 0) & (origin < tps))
            def _():
                for part in range(len(tok_parts)):
                    tok_copy(1, origin, part, way, hop, device).wait_send()
    for way, (there, device) in enumerate((code_up, code_down)):
        sign = 1 - 2 * way
        for hop in range(chips):
            origin = chip - sign * hop
            owner = rep - 2 * sign * hop
            here = (origin >= 0) & (origin < chips)
            if hop < chips - 1:
                @pl.when(there & here)
                def _():
                    scale_copy(1, owner, way, hop, device).wait_send()
                    for part in range(code_parts):
                        code_copy(1, owner, part, way, hop, device).wait_send()
            if hop or not way:
                @pl.when(here)
                def _():
                    scale_copy(1, owner, 2 + way, hop, partner).wait_send()
                    for part in range(code_parts):
                        code_copy(1, owner, part, 2 + way, hop, partner).wait_send()


def local(tps, reps, tokens, base_weight, delta_codes, delta_scales, replica_variant, block_home):
    slots, col_blocks = delta_scales.shape
    rows, depth = tokens.shape
    width = base_weight.shape[1]
    block = delta_codes.shape[0] // slots
    sizes = (depth // 2, 3 * depth // 8, depth // 8)
    tok_parts = tuple((sum(sizes[:i]), size) for i, size in enumerate(sizes))
    code_parts = max(1, 8 // reps)
    codes = delta_codes.reshape(slots, block, width)
    operands = [
        pltpu.with_memory_space_constraint(x, pltpu.HBM)
        for x in (replica_variant, block_home, delta_scales.T, tokens, base_weight, codes)
    ]
    dma = pltpu.SemaphoreType.DMA
    chips = reps // 2
    return pl.pallas_call(
        functools.partial(kernel, (tps, reps, tok_parts, code_parts, slots, block, width)),
        out_shape=jax.ShapeDtypeStruct((tps * rows, width), jnp.bfloat16),
        in_specs=[pl.BlockSpec(memory_space=pl.ANY)] * 6,
        out_specs=pl.BlockSpec(memory_space=pltpu.VMEM),
        scratch_shapes=[
            pltpu.SMEM(replica_variant.shape, jnp.int32),
            pltpu.SMEM(block_home.shape, jnp.int32),
            pltpu.VMEM((tps, rows, depth), jnp.bfloat16),
            pltpu.VMEM((reps * slots, block, width), jnp.bfloat16),
            pltpu.VMEM((depth, width), jnp.bfloat16),
            pltpu.VMEM((reps, col_blocks, slots), jnp.bfloat16),
            pltpu.VMEM((reps * slots, width), jnp.float32),
            pltpu.VMEM((tps * rows, width), jnp.float32),
            dma((2, tps, len(tok_parts))),
            dma((tps, len(tok_parts))),
            dma((4, chips, code_parts)),
            dma((reps, code_parts)),
            dma((4, chips)),
            dma((reps,)),
            dma((6,)),
        ],
        compiler_params=pltpu.CompilerParams(
            collective_id=0, has_side_effects=True, vmem_limit_bytes=48 * 1024 * 1024
        ),
    )(*operands)


def solution(mesh):
    in_specs = (
        P(("groups", "rep", "tp"), None),
        P(None, "tp"),
        P(("groups", "rep"), "tp"),
        P(("groups", "rep"), "tp"),
        P("groups"),
        P("groups", None),
    )
    out_specs = P(("groups", "rep"), "tp")
    body = functools.partial(local, mesh.shape["tp"], mesh.shape["rep"])
    return jax.shard_map(body, mesh=mesh, in_specs=in_specs, out_specs=out_specs, check_vma=False)
```
